1024 devices in a mesh: ctx: 64 (over y_hi, x, core), head: 16 (over y_lo, z).
Axes of the slice: x: 8, y: 8 (y_hi: 4, y_lo: 2; y = y_hi * 2 + y_lo), z: 8, core: 2. Of those that a mesh axis runs over, the one named last changes fastest.
Arguments:
- q_att: bfloat16 [16384, 2048], P('ctx', 'head'), may hold values from -6 to 6
- k_att: bfloat16 [16384, 2048], P('ctx', 'head'), may hold values from -6 to 6
- v_att: bfloat16 [16384, 2048], P('ctx', 'head'), may hold values from -6 to 6
- norm_gain: float32 [2048], P('head'), may hold values from 0.25 to 1.75
- hy_q: bfloat16 [16384, 2048], P('ctx', 'head'), may hold values from -6 to 6
- hy_k: bfloat16 [16384, 2048], P('ctx', 'head'), may hold values from -6 to 6
- feat_w: float32 [3, 7, 2048], P(None, None, 'head'), may hold values from -2 to 2
- mr_filt: float32 [128, 128], P(None, 'head'), may hold values from -0.5 to 0.5
- cotangent: bfloat16 [16384, 2048], P('ctx', 'head'), may hold values from -6 to 6
Outputs:
- output: bfloat16 [16384, 2048], P('ctx', 'head')
- grad_q: bfloat16 [16384, 2048], P('ctx', 'head')
- grad_k: bfloat16 [16384, 2048], P('ctx', 'head')
- grad_v: bfloat16 [16384, 2048], P('ctx', 'head')
The draws below stay inside these ranges and needn't reach their ends.
All inputs are finite; a program needn't handle non-finite values.
Results may differ from the reference program's by a relative error of at most 0.019.
Values may be sent and summed in bfloat16 or wider, within the bound.
No kernel may reach another device: no remote copies, remote signals or barrier semaphores. Data moves between devices by JAX's collectives and lax.ppermute only.
A program may use at most 64 MiB of HBM per device.

```python
import math
import jax
import jax.numpy as jnp
from jax import lax

HD = 128
GROUP_CH = 16
FEAT = 7
FILT = 128
TOKENS = 16384
WIDTH = 2048


def attention_pair(key):
    queries = jnp.clip(jax.random.normal(jax.random.fold_in(key, 101), (TOKENS, WIDTH), jnp.float32), -6.0, 6.0)
    keys_drawn = jnp.clip(jax.random.normal(jax.random.fold_in(key, 102), (TOKENS, WIDTH), jnp.float32), -6.0, 6.0)
    return (queries, keys_drawn)


def draw_q_att(key, part):
    return attention_pair(key)[0].astype(jnp.bfloat16)


def draw_k_att(key, part):
    return attention_pair(key)[1].astype(jnp.bfloat16)


def draw_v_att(key, part):
    channel = jnp.arange(WIDTH) // HD
    position = channel.astype(jnp.float32) / max(WIDTH // HD - 1, 1)
    base = jnp.clip(jax.random.normal(key, (TOKENS, WIDTH), jnp.float32), -3.4, 3.4)
    return (base * jnp.power(3.0, 0.5 * position)[None, :]).astype(jnp.bfloat16)


def shard_levels(key, shape, cuts, smallest, high):
    factor_of = 1.0
    for dim, shards_of in cuts:
        steps = jax.random.uniform(jax.random.fold_in(jax.random.fold_in(key, 6), dim), (shards_of,), jnp.float32, smallest / len(cuts), high / len(cuts))
        factor_of = factor_of * jnp.repeat(jnp.exp(steps), shape[dim] // shards_of).reshape((-1,) + (1,) * (len(shape) - 1 - dim))
    return factor_of


def noise(own_key, extent, deviation, most, split=(), kind=jnp.bfloat16):
    array = deviation * jax.random.normal(own_key, extent, jnp.float32)
    if split:
        array = array * shard_levels(own_key, extent, split, -0.22, 0.18)
    return jnp.clip(array, -most, most).astype(kind)


def setup_inputs(seed: int = 0) -> dict:
    seeds = jax.random.split(jax.random.key(seed), 10)
    q_att = draw_q_att(jax.random.fold_in(seeds[9], 71), 0)
    k_att = draw_k_att(jax.random.fold_in(seeds[9], 71), 0)
    v_att = draw_v_att(jax.random.fold_in(seeds[9], 71), 0)
    norm_gain = jnp.clip(1.0 + 0.15 * jax.random.normal(seeds[3], (WIDTH,), jnp.float32), 0.25, 1.75)
    hy_q = noise(seeds[4], (TOKENS, WIDTH), 1.0, 6.0, ((0, 64), (1, 16)))
    hy_k = noise(seeds[5], (TOKENS, WIDTH), 1.0, 6.0, ((0, 64), (1, 16)))
    feat_w = noise(seeds[6], (3, FEAT, WIDTH), FEAT ** -0.5, 2.0, ((2, 16),), jnp.float32)
    mr_filt = noise(seeds[7], (FILT, WIDTH // GROUP_CH), FILT ** -0.5, 0.5, ((1, 16),), jnp.float32)
    cotangent = noise(seeds[8], (TOKENS, WIDTH), 1.0, 6.0, ((0, 64), (1, 16)))
    return {"q_att": q_att, "k_att": k_att, "v_att": v_att, "norm_gain": norm_gain, "hy_q": hy_q, "hy_k": hy_k, "feat_w": feat_w, "mr_filt": mr_filt, "cotangent": cotangent}


NEGATIVE = -1e+30
EPSILON = 1e-06

def attention(queries, keys, values):
    total_rows, width = queries.shape
    heads = width // HD
    query_heads = queries.astype(jnp.float32).reshape(total_rows, heads, HD)
    key_heads = keys.astype(jnp.float32).reshape(total_rows, heads, HD)
    value_heads = values.astype(jnp.float32).reshape(total_rows, heads, HD)
    block = math.gcd(total_rows, 256)
    key_pos = jnp.arange(total_rows, dtype=jnp.int32)

    def one_block(begin):
        query_block = lax.dynamic_slice_in_dim(query_heads, begin.astype(jnp.int32), block, 0)
        scores = jnp.einsum('thd,phd->htp', query_block, key_heads) / math.sqrt(HD)
        query_pos = begin.astype(jnp.int32) + jnp.arange(block, dtype=jnp.int32)
        allowed = key_pos[None, :] <= query_pos[:, None]
        scores = jnp.where(allowed[None], scores, NEGATIVE)
        top = lax.optimization_barrier(jnp.max(scores, axis=-1, keepdims=True))
        probs = jnp.where(allowed[None], jnp.exp(scores - top), 0.0)
        totals = lax.optimization_barrier(jnp.sum(probs, axis=-1))
        weights = probs.astype(jnp.bfloat16).astype(jnp.float32)
        summed = jnp.einsum('htp,phd->thd', weights, value_heads)
        result = summed / jnp.transpose(totals)[:, :, None]
        return result.reshape(block, width).astype(jnp.bfloat16)
    starts = jnp.arange(total_rows // block, dtype=jnp.int32) * block
    return lax.map(one_block, starts).reshape(total_rows, width)

def causal_feature(stream, taps):
    width = taps.shape[0]
    count = stream.shape[0]
    padded = jnp.pad(stream.astype(jnp.float32), ((width - 1, 0), (0, 0)))
    total = jnp.zeros(stream.shape, jnp.float32)
    for lag in range(width):
        total = total + taps[lag] * padded[width - 1 - lag:width - 1 - lag + count]
    return total

def feature_back(grad, taps):
    width = taps.shape[0]
    count = grad.shape[0]
    padded = jnp.pad(grad.astype(jnp.float32), ((0, width - 1), (0, 0)))
    total = jnp.zeros(grad.shape, jnp.float32)
    for lag in range(width):
        total = total + taps[lag] * padded[lag:lag + count]
    return total

def long_conv(mixed, taps_ch):
    length = taps_ch.shape[0]
    count = mixed.shape[0]
    padded = jnp.pad(mixed, ((length - 1, 0), (0, 0)))

    def add_tap(lag, total):
        begin = (length - 1 - lag).astype(jnp.int32)
        return total + taps_ch[lag] * lax.dynamic_slice_in_dim(padded, begin, count, 0)
    return lax.fori_loop(0, length, add_tap, jnp.zeros(mixed.shape, jnp.float32))

def long_back(grad, taps_ch):
    length = taps_ch.shape[0]
    count = grad.shape[0]
    padded = jnp.pad(grad, ((0, length - 1), (0, 0)))

    def add_tap(lag, total):
        begin = lag.astype(jnp.int32)
        return total + taps_ch[lag] * lax.dynamic_slice_in_dim(padded, begin, count, 0)
    return lax.fori_loop(0, length, add_tap, jnp.zeros(grad.shape, jnp.float32))

def reference(q_att, k_att, v_att, norm_gain, hy_q, hy_k, feat_w, mr_filt, cotangent):
    attended = attention(q_att, k_att, v_att).astype(jnp.float32)
    mean_sq = lax.optimization_barrier(jnp.mean(attended * attended, axis=1, keepdims=True))
    value_stream = (attended * lax.rsqrt(mean_sq + EPSILON) * norm_gain).astype(jnp.bfloat16)
    q_feat = causal_feature(hy_q, feat_w[0]).astype(jnp.bfloat16).astype(jnp.float32)
    k_feat = causal_feature(hy_k, feat_w[1]).astype(jnp.bfloat16).astype(jnp.float32)
    v_feat = causal_feature(value_stream, feat_w[2]).astype(jnp.bfloat16).astype(jnp.float32)
    mixed = (k_feat * v_feat).astype(jnp.bfloat16).astype(jnp.float32)
    taps_ch = jnp.repeat(mr_filt, GROUP_CH, axis=1)
    signal = long_conv(mixed, taps_ch)
    output = (q_feat * signal).astype(jnp.bfloat16)
    grad_out = cotangent.astype(jnp.float32)
    d_signal = (grad_out * q_feat).astype(jnp.bfloat16).astype(jnp.float32)
    d_qf = (grad_out * signal).astype(jnp.bfloat16)
    d_mixed = long_back(d_signal, taps_ch)
    d_kf = (d_mixed * v_feat).astype(jnp.bfloat16)
    d_vf = (d_mixed * k_feat).astype(jnp.bfloat16)
    grad_q = feature_back(d_qf, feat_w[0]).astype(jnp.bfloat16)
    grad_k = feature_back(d_kf, feat_w[1]).astype(jnp.bfloat16)
    grad_v = feature_back(d_vf, feat_w[2]).astype(jnp.bfloat16)
    return (output, grad_q, grad_k, grad_v)
```

```python
import functools
import math

import jax
import jax.numpy as jnp
from jax import lax
from jax.experimental import pallas as pl
from jax.experimental.pallas import tpu as pltpu
from jax.sharding import Mesh, PartitionSpec as P

HD = 128
GROUP_CH = 16
FEAT = 7
FILT = 128
BLOCK = 256
NEGATIVE = -1e30
EPSILON = 1e-06
LOG2E = 1.4426950408889634
FACTOR = LOG2E / math.sqrt(HD)
EXT = 144
F32 = jnp.float32
BF16 = jnp.bfloat16


VM = pl.BlockSpec(memory_space=pltpu.VMEM)
SM = pl.BlockSpec(memory_space=pltpu.SMEM)


def rounded(x):
    return x.astype(BF16).astype(F32)


def dot(a, b, dims):
    return lax.dot_general(a, b, (dims, ((), ())), preferred_element_type=F32)


def to_rows(x):
    i = lax.broadcasted_iota(jnp.int32, (128, 128), 0)
    j = lax.broadcasted_iota(jnp.int32, (128, 128), 1)
    return jnp.sum(jnp.where(i == j, x, 0.0), axis=0, keepdims=True)


def stacked(rows, height):
    at = lax.broadcasted_iota(jnp.int32, (height, 128), 0)
    out = jnp.zeros((height, 128), F32)
    for i, row in enumerate(rows):
        out = jnp.where(at == i, row, out)
    return out


def attend(info, q_ref, own_ref, oth_ref, o_ref, k_ref, v_ref, acc_ref, m_ref, s_ref, t_ref, d_ref):
    plane, column, core = info[0], info[1], info[2]

    def fill(p, c):
        for half, src in ((0, own_ref), (1, oth_ref)):
            keys = src[p, 0:256, :]
            k_ref[p, 256 * half : 256 * half + 256, :] = keys
            v_ref[p, 256 * half : 256 * half + 256, :] = jnp.concatenate(
                [src[p, 256:512, :], jnp.ones((256, 128), BF16)], axis=1
            )
        return c

    lax.fori_loop(0, plane + 1, fill, 0)

    def split(b, c):
        acc_ref[b] = jnp.zeros((256, 256), F32)
        m_ref[b] = jnp.full((256, 128), NEGATIVE, F32)
        return c

    lax.fori_loop(0, 8, split, 0)

    i = lax.broadcasted_iota(jnp.int32, (256, 256), 0)
    j = lax.broadcasted_iota(jnp.int32, (256, 256), 1)
    d_ref[...] = j - i

    def scores(n, b, p, masked):
        s = dot(q_ref[b], k_ref[p], ((1,), (1,))) * FACTOR
        if masked:
            bound = jnp.where(b > column, 512, jnp.where(b == column, 0, -512))
            seen = jnp.where(b > column, 1, jnp.where(b == column, core, 0))
            s = jnp.concatenate(
                [
                    jnp.where(d_ref[...] <= bound, s[:, 0:256], NEGATIVE),
                    jnp.where(jnp.full((256, 256), seen, jnp.int32) == 1, s[:, 256:512], NEGATIVE),
                ],
                axis=1,
            )
        s_ref[n] = s
        t_ref[n] = jnp.broadcast_to(jnp.max(s, axis=1, keepdims=True), (256, 128))

    def update(n, b, p):
        old = m_ref[b]
        new = jnp.maximum(old, rounded(t_ref[n]))
        m_ref[b] = new
        scale = jnp.exp2(old - new)
        e = jnp.concatenate([jnp.exp2(s_ref[n, :, 128 * k : 128 * k + 128] - new) for k in range(4)], axis=1)
        add = dot(e.astype(BF16), v_ref[p], ((1,), (0,)))
        acc_ref[b, :, 0:128] = acc_ref[b, :, 0:128] * scale + add[:, 0:128]
        acc_ref[b, :, 128:256] = acc_ref[b, :, 128:256] * scale + add[:, 128:256]

    def some(first, p, masked):
        for n in range(8):
            scores(n, first + n, p, masked)
            if n:
                update(n - 1, first + n - 1, p)
        update(8 - 1, first + 8 - 1, p)

    def same(g, c):
        @pl.when(8 * (g + 1) > column)
        def _():
            some(8 * g, 0, True)

        return c

    lax.fori_loop(0, 8 // 8, same, 0)

    def past(g, c):
        some(8 * lax.rem(g, 8 // 8), 1 + lax.div(g, 8 // 8), False)
        return c

    lax.fori_loop(0, plane * (8 // 8), past, 0)

    def emit(b, c):
        o_ref[b, 0:256, :] = acc_ref[b, :, 0:128].astype(BF16)
        tops, high, low = [], [], []
        for h in range(2):
            part = slice(128 * h, 128 * h + 128)
            tops.append(to_rows(m_ref[b, part, :]))
            mass = to_rows(acc_ref[b, part, 128:256])
            upper = rounded(mass)
            high.append(upper)
            low.append(mass - upper)
        o_ref[b, 256:272, :] = stacked(tops + high + low, 16).astype(BF16)
        return c

    lax.fori_loop(0, 8, emit, 0)


def combine(msg_ref, a_ref, s_ref):
    copies = s_ref.shape[0]
    n = msg_ref.shape[0]
    stats = [msg_ref[i, 256:272, :].astype(F32) for i in range(n)]
    sums = []
    for h in range(2):
        tops = [s[h : h + 1] for s in stats]
        totals = [s[2 + h : 3 + h] + s[4 + h : 5 + h] for s in stats]
        top = functools.reduce(jnp.maximum, tops)
        weights = [jnp.exp2(t - top) for t in tops]
        total = sum(w * t for w, t in zip(weights, totals))
        shares = jnp.transpose(stacked([w / total for w in weights], 128))
        out = jnp.zeros((128, 128), F32)
        for i in range(n):
            out = out + shares[:, i : i + 1] * msg_ref[i, 128 * h : 128 * h + 128, :].astype(F32)
        out = out.astype(BF16)
        a_ref[128 * h : 128 * h + 128, :] = out
        square = out.astype(F32) * out.astype(F32)
        upper = square.astype(BF16)
        lower = (square - upper.astype(F32)).astype(BF16)
        ones = jnp.ones((8, 128), BF16)
        sums.append((dot(ones, upper, ((1,), (1,))) + dot(ones, lower, ((1,), (1,))))[0:1])
    both = stacked(sums, 8)
    for i in range(copies):
        s_ref[i] = both


def normalize(a_ref, s_ref, g_ref, v_ref, end_ref, begin_ref):
    n = s_ref.shape[0]
    total = functools.reduce(jnp.add, [s_ref[i] for i in range(n)])
    scale = lax.rsqrt(total * (1.0 / (n * 128)) + EPSILON)
    column = jnp.transpose(jnp.concatenate([scale, jnp.zeros((120, 128), F32)], axis=0))
    for h in range(2):
        part = slice(128 * h, 128 * h + 128)
        v_ref[part, :] = (a_ref[part, :].astype(F32) * column[:, h : h + 1] * g_ref[...]).astype(BF16)
    end_ref[...] = v_ref[256 - EXT : 256, :]
    begin_ref[...] = v_ref[0:16, :]


def picked(stack, rows):
    lane = lax.broadcasted_iota(jnp.int32, (rows, 128), 1) // GROUP_CH
    out = stack[0:rows]
    for g in range(1, 8):
        out = jnp.where(lane == g, stack[g * rows : (g + 1) * rows], out)
    return out


def banded(bands, data_ref):
    out = []
    for b in range(2):
        out.append(picked(dot(bands[...], data_ref[128 * b : 128 * b + 256, :], ((1,), (0,))), 128))
    tail = jnp.concatenate([bands[128 * g : 128 * g + 16, :] for g in range(8)], axis=0)
    out.append(picked(dot(tail, data_ref[256:512, :], ((1,), (0,))), 16)[0:8])
    return out


def prepare(
    q_ref, k_ref, c_ref, before_ref, after_ref, w_ref, front_ref, back_ref,
    t_ref, kf_ref, qf_ref, ce_ref, dm_ref,
    bt_ref, x_ref, y_ref, z_ref,
):
    for g in range(8):
        row = jnp.broadcast_to(front_ref[g : g + 1, :], (128, 256))
        t_ref[128 * g : 128 * g + 128, :] = pltpu.roll(row, 0, 1, stride=1, stride_axis=0).astype(BF16)
        row = jnp.broadcast_to(back_ref[g : g + 1, :], (128, 256))
        bt_ref[128 * g : 128 * g + 128, :] = pltpu.roll(row, 0, 1, stride=1, stride_axis=0).astype(BF16)
    x_ref[0:144, :] = before_ref[16:160, :].astype(F32)
    x_ref[144:400, :] = k_ref[...].astype(F32)
    x_ref[400:416, :] = after_ref[288:304, :].astype(F32)
    total = jnp.zeros((392, 128), F32)
    for lag in range(FEAT):
        total = total + w_ref[1, lag : lag + 1, :] * x_ref[16 - lag : 408 - lag, :]
    kf_ref[...] = rounded(total)
    y_ref[0:16, :] = before_ref[0:16, :].astype(F32)
    y_ref[16:272, :] = q_ref[...].astype(F32)
    y_ref[272:416, :] = after_ref[0:144, :].astype(F32)
    total = jnp.zeros((392, 128), F32)
    for lag in range(FEAT):
        total = total + w_ref[0, lag : lag + 1, :] * y_ref[16 - lag : 408 - lag, :]
    qf = rounded(total)
    qf_ref[...] = qf[0:264]
    x_ref[0:256, :] = c_ref[...].astype(F32)
    x_ref[256:400, :] = after_ref[144:288, :].astype(F32)
    ce_ref[...] = x_ref[0:264, :]
    z_ref[0:384, :] = (x_ref[0:384, :] * qf[0:384]).astype(BF16)
    last = jnp.concatenate([x_ref[384:392, :] * qf[384:392], jnp.zeros((8, 128), F32)], axis=0)
    z_ref[384:400, :] = last.astype(BF16)
    z_ref[400:512, :] = jnp.zeros((112, 128), BF16)
    for b, part in enumerate(banded(bt_ref, z_ref)):
        dm_ref[128 * b : 128 * b + part.shape[0], :] = part


def finish(
    v_ref, before_ref, after_ref, w_ref, t_ref, kf_ref, qf_ref, ce_ref, dm_ref,
    o_ref, gq_ref, gk_ref, gv_ref,
    x_ref, z_ref, a_ref, b_ref, c_ref,
):
    x_ref[0:144, :] = before_ref[...].astype(F32)
    x_ref[144:400, :] = v_ref[...].astype(F32)
    x_ref[400:416, :] = after_ref[...].astype(F32)
    total = jnp.zeros((392, 128), F32)
    for lag in range(FEAT):
        total = total + w_ref[2, lag : lag + 1, :] * x_ref[16 - lag : 408 - lag, :]
    vf = rounded(total)
    kf = kf_ref[...]
    mixed = kf * vf
    z_ref[0:384, :] = mixed[0:384].astype(BF16)
    last = jnp.concatenate([mixed[384:392], jnp.zeros((8, 128), F32)], axis=0)
    z_ref[384:400, :] = last.astype(BF16)
    z_ref[400:512, :] = jnp.zeros((112, 128), BF16)
    for b, signal in enumerate(banded(t_ref, z_ref)):
        part = slice(128 * b, 128 * b + signal.shape[0])
        if b < 2:
            o_ref[part, :] = (qf_ref[part, :] * signal).astype(BF16)
        a_ref[part, :] = rounded(ce_ref[part, :] * signal)
    b_ref[...] = rounded(dm_ref[...] * vf[128:392])
    c_ref[...] = rounded(dm_ref[...] * kf[128:392])
    for i, (src, dst) in enumerate(((a_ref, gq_ref), (b_ref, gk_ref), (c_ref, gv_ref))):
        total = jnp.zeros((256, 128), F32)
        for lag in range(FEAT):
            total = total + w_ref[i, lag : lag + 1, :] * src[lag : lag + 256, :]
        dst[...] = total.astype(BF16)


def shape(dims, dtype=BF16):
    return jax.ShapeDtypeStruct(dims, dtype)


def call(body, outs, args, scratch=(), specs=None, flops=0, size=1 << 20, flags=None):
    single = not isinstance(outs, (list, tuple))
    return pl.pallas_call(
        body,
        out_shape=outs,
        in_specs=specs or [VM] * len(args),
        out_specs=VM if single else [VM] * len(outs),
        scratch_shapes=list(scratch),
        cost_estimate=pl.CostEstimate(flops=flops, bytes_accessed=size, transcendentals=0),
        compiler_params=pltpu.CompilerParams(flags=flags) if flags else None,
    )(*args)


CTX = ("y_hi", "x", "core")
HEAD = ("y_lo", "z")


def neighbour(block, distance):
    n = lax.axis_size(CTX)
    return lax.ppermute(block, CTX, [(i, i + distance) for i in range(n) if 0 <= i + distance < n])


def per_device(q_att, k_att, v_att, norm_gain, hy_q, hy_k, feat_w, mr_filt, cotangent):
    info = jnp.stack([lax.axis_index("y_hi"), lax.axis_index("x"), lax.axis_index("core"), 0]).astype(jnp.int32)
    rows = lax.all_to_all(jnp.broadcast_to(q_att[None], (8, BLOCK, HD)), "x", 0, 0, tiled=True)
    both = jnp.concatenate([k_att, v_att], axis=0)
    came = [lax.ppermute(both, "y_hi", [(i, i + d) for i in range(4 - d)]) for d in (1, 2, 3)]
    own = jnp.stack([both] + came)
    other = lax.ppermute(own, "core", [(0, 1), (1, 0)])
    before = neighbour(jnp.concatenate([hy_q[-16:], hy_k[-EXT:]], axis=0), 1)
    after = neighbour(jnp.concatenate([hy_q[:EXT], cotangent[:EXT], hy_k[:16]], axis=0), -1)

    taps = mr_filt.T
    zero = jnp.zeros((8, 128), F32)
    back = jnp.concatenate([taps, zero], axis=1)
    front = jnp.concatenate([zero[:, :1], taps[:, ::-1], zero[:, 1:]], axis=1)
    bands, kf, qf, ce, dm = call(
        prepare,
        [shape((1024, 256)), shape((392, 128), F32), shape((264, 128), F32), shape((264, 128), F32), shape((264, 128), F32)],
        (hy_q, hy_k, cotangent, before, after, feat_w, front, back),
        [pltpu.VMEM((1024, 256), BF16), pltpu.VMEM((416, 128), F32), pltpu.VMEM((416, 128), F32), pltpu.VMEM((512, 128), BF16)],
        flops=10**9,
    )
    info, rows, own, other, bands, kf, qf, ce, dm = lax.optimization_barrier(
        (info, rows, own, other, bands, kf, qf, ce, dm)
    )
    partial = call(
        attend,
        shape((8, 272, 128)),
        (info, rows, own, other),
        [
            pltpu.VMEM((4, 512, 128), BF16),
            pltpu.VMEM((4, 512, 256), BF16),
            pltpu.VMEM((8, 256, 256), F32),
            pltpu.VMEM((8, 256, 128), F32),
            pltpu.VMEM((8, 256, 512), F32),
            pltpu.VMEM((8, 256, 128), F32),
            pltpu.VMEM((256, 256), jnp.int32),
        ],
        specs=[SM, VM, VM, VM],
        flops=4 * 10**9,
    )
    parts = lax.all_to_all(partial, "x", 0, 0, tiled=True)
    attended, sums = call(combine, [shape((256, 128)), shape((16, 8, 128), F32)], (parts,))
    squares = lax.all_to_all(sums, HEAD, 0, 0, tiled=True)
    value, end, begin = call(
        normalize, [shape((256, 128)), shape((EXT, 128)), shape((16, 128))], (attended, squares, norm_gain[None])
    )
    v_before = neighbour(end, 1)
    v_after = neighbour(begin, -1)
    return tuple(
        call(
            finish,
            [shape((256, 128))] * 4,
            (value, v_before, v_after, feat_w, bands, kf, qf, ce, dm),
            [pltpu.VMEM((416, 128), F32), pltpu.VMEM((512, 128), BF16)] + [pltpu.VMEM((264, 128), F32)] * 3,
        )
    )


def solution(mesh):
    fine = Mesh(mesh.devices.reshape(4, 8, 2, 2, 8), CTX + HEAD)
    tokens = P(CTX, HEAD)
    placed = (tokens, tokens, tokens, P(HEAD), tokens, tokens, P(None, None, HEAD), P(None, HEAD), tokens)
    return jax.shard_map(per_device, mesh=fine, in_specs=placed, out_specs=(tokens,) * 4, check_vma=False)
```

```python
import functools
import math

import jax
import jax.numpy as jnp
from jax import lax
from jax.experimental import pallas as pl
from jax.experimental.pallas import tpu as pltpu
from jax.sharding import Mesh, PartitionSpec as P

HD = 128
GROUP_CH = 16
FEAT = 7
FILT = 128
BLOCK = 256
NEGATIVE = -1e30
EPSILON = 1e-06
LOG2E = 1.4426950408889634
FACTOR = LOG2E / math.sqrt(HD)
EXT = 144
F32 = jnp.float32
BF16 = jnp.bfloat16


VM = pl.BlockSpec(memory_space=pltpu.VMEM)
SM = pl.BlockSpec(memory_space=pltpu.SMEM)


def rounded(x):
    return x.astype(BF16).astype(F32)


def dot(a, b, dims):
    return lax.dot_general(a, b, (dims, ((), ())), preferred_element_type=F32)


def to_rows(x):
    i = lax.broadcasted_iota(jnp.int32, (128, 128), 0)
    j = lax.broadcasted_iota(jnp.int32, (128, 128), 1)
    return jnp.sum(jnp.where(i == j, x, 0.0), axis=0, keepdims=True)


def stacked(rows, height):
    at = lax.broadcasted_iota(jnp.int32, (height, 128), 0)
    out = jnp.zeros((height, 128), F32)
    for i, row in enumerate(rows):
        out = jnp.where(at == i, row, out)
    return out


def attend(info, q_ref, own_ref, oth_ref, o_ref, k_ref, v_ref, acc_ref, m_ref, s_ref, t_ref, d_ref):
    plane, column, core = info[0], info[1], info[2]

    def fill(p, c):
        for half, src in ((0, own_ref), (1, oth_ref)):
            keys = src[p, 0:256, :]
            k_ref[p, 256 * half : 256 * half + 256, :] = keys
            v_ref[p, 256 * half : 256 * half + 256, :] = jnp.concatenate(
                [src[p, 256:512, :], jnp.ones((256, 128), BF16)], axis=1
            )
        return c

    lax.fori_loop(0, plane + 1, fill, 0)

    def split(b, c):
        acc_ref[b] = jnp.zeros((256, 256), F32)
        m_ref[b] = jnp.full((256, 128), NEGATIVE, F32)
        return c

    lax.fori_loop(0, 8, split, 0)

    i = lax.broadcasted_iota(jnp.int32, (256, 256), 0)
    j = lax.broadcasted_iota(jnp.int32, (256, 256), 1)
    d_ref[...] = j - i

    def scores(n, b, p, masked):
        s = dot(q_ref[b], k_ref[p], ((1,), (1,))) * FACTOR
        if masked:
            bound = jnp.where(b > column, 512, jnp.where(b == column, 0, -512))
            seen = jnp.where(b > column, 1, jnp.where(b == column, core, 0))
            s = jnp.concatenate(
                [
                    jnp.where(d_ref[...] <= bound, s[:, 0:256], NEGATIVE),
                    jnp.where(jnp.full((256, 256), seen, jnp.int32) == 1, s[:, 256:512], NEGATIVE),
                ],
                axis=1,
            )
        s_ref[n] = s
        t_ref[n] = jnp.broadcast_to(jnp.max(s, axis=1, keepdims=True), (256, 128))

    def update(n, b, p):
        old = m_ref[b]
        new = jnp.maximum(old, rounded(t_ref[n]))
        m_ref[b] = new
        scale = jnp.exp2(old - new)
        e = jnp.concatenate([jnp.exp2(s_ref[n, :, 128 * k : 128 * k + 128] - new) for k in range(4)], axis=1)
        add = dot(e.astype(BF16), v_ref[p], ((1,), (0,)))
        acc_ref[b, :, 0:128] = acc_ref[b, :, 0:128] * scale + add[:, 0:128]
        acc_ref[b, :, 128:256] = acc_ref[b, :, 128:256] * scale + add[:, 128:256]

    def some(first, p, masked):
        for n in range(8):
            scores(n, first + n, p, masked)
            if n:
                update(n - 1, first + n - 1, p)
        update(8 - 1, first + 8 - 1, p)

    def same(g, c):
        @pl.when(8 * (g + 1) > column)
        def _():
            some(8 * g, 0, True)

        return c

    lax.fori_loop(0, 8 // 8, same, 0)

    def past(g, c):
        some(8 * lax.rem(g, 8 // 8), 1 + lax.div(g, 8 // 8), False)
        return c

    lax.fori_loop(0, plane * (8 // 8), past, 0)

    def emit(b, c):
        o_ref[b, 0:256, :] = acc_ref[b, :, 0:128].astype(BF16)
        tops, high, low = [], [], []
        for h in range(2):
            part = slice(128 * h, 128 * h + 128)
            tops.append(to_rows(m_ref[b, part, :]))
            mass = to_rows(acc_ref[b, part, 128:256])
            upper = rounded(mass)
            high.append(upper)
            low.append(mass - upper)
        o_ref[b, 256:272, :] = stacked(tops + high + low, 16).astype(BF16)
        return c

    lax.fori_loop(0, 8, emit, 0)


def combine(msg_ref, a_ref, s_ref):
    copies = s_ref.shape[0]
    n = msg_ref.shape[0]
    stats = [msg_ref[i, 256:272, :].astype(F32) for i in range(n)]
    sums = []
    for h in range(2):
        tops = [s[h : h + 1] for s in stats]
        totals = [s[2 + h : 3 + h] + s[4 + h : 5 + h] for s in stats]
        top = functools.reduce(jnp.maximum, tops)
        weights = [jnp.exp2(t - top) for t in tops]
        total = sum(w * t for w, t in zip(weights, totals))
        shares = jnp.transpose(stacked([w / total for w in weights], 128))
        out = jnp.zeros((128, 128), F32)
        for i in range(n):
            out = out + shares[:, i : i + 1] * msg_ref[i, 128 * h : 128 * h + 128, :].astype(F32)
        out = out.astype(BF16)
        a_ref[128 * h : 128 * h + 128, :] = out
        square = out.astype(F32) * out.astype(F32)
        upper = square.astype(BF16)
        lower = (square - upper.astype(F32)).astype(BF16)
        ones = jnp.ones((8, 128), BF16)
        sums.append((dot(ones, upper, ((1,), (1,))) + dot(ones, lower, ((1,), (1,))))[0:1])
    both = stacked(sums, 8)
    for i in range(copies):
        s_ref[i] = both


def normalize(a_ref, s_ref, g_ref, v_ref, end_ref, begin_ref):
    n = s_ref.shape[0]
    total = functools.reduce(jnp.add, [s_ref[i] for i in range(n)])
    scale = lax.rsqrt(total * (1.0 / (n * 128)) + EPSILON)
    column = jnp.transpose(jnp.concatenate([scale, jnp.zeros((120, 128), F32)], axis=0))
    for h in range(2):
        part = slice(128 * h, 128 * h + 128)
        v_ref[part, :] = (a_ref[part, :].astype(F32) * column[:, h : h + 1] * g_ref[...]).astype(BF16)
    end_ref[...] = v_ref[256 - EXT : 256, :]
    begin_ref[...] = v_ref[0:16, :]


def picked(stack, rows):
    lane = lax.broadcasted_iota(jnp.int32, (rows, 128), 1) // GROUP_CH
    out = stack[0:rows]
    for g in range(1, 8):
        out = jnp.where(lane == g, stack[g * rows : (g + 1) * rows], out)
    return out


def banded(bands, data_ref):
    out = []
    for b in range(2):
        out.append(picked(dot(bands[...], data_ref[128 * b : 128 * b + 256, :], ((1,), (0,))), 128))
    tail = jnp.concatenate([bands[128 * g : 128 * g + 16, :] for g in range(8)], axis=0)
    out.append(picked(dot(tail, data_ref[256:512, :], ((1,), (0,))), 16)[0:8])
    return out


def prepare(
    q_ref, k_ref, c_ref, before_ref, after_ref, w_ref, f_ref, gain_ref,
    t_ref, kf_ref, qf_ref, ce_ref, dm_ref, g_ref,
    bt_ref, x_ref, y_ref, z_ref,
):
    i = lax.broadcasted_iota(jnp.int32, (128, 128), 0)
    j = lax.broadcasted_iota(jnp.int32, (128, 128), 1)
    taps = f_ref[...].astype(BF16)
    front = dot(taps, (i + j == 128).astype(BF16), ((0,), (0,)))
    first = jnp.where(lax.broadcasted_iota(jnp.int32, (8, 128), 1) == 0, dot(taps, (i == 0).astype(BF16), ((0,), (0,))), 0.0)
    back = dot(taps, (i == j).astype(BF16), ((0,), (0,)))
    front = jnp.concatenate([front, first], axis=1)
    back = jnp.concatenate([back, jnp.zeros((8, 128), F32)], axis=1)
    for g in range(8):
        row = jnp.broadcast_to(front[g : g + 1, :], (128, 256))
        t_ref[128 * g : 128 * g + 128, :] = pltpu.roll(row, 0, 1, stride=1, stride_axis=0).astype(BF16)
        row = jnp.broadcast_to(back[g : g + 1, :], (128, 256))
        bt_ref[128 * g : 128 * g + 128, :] = pltpu.roll(row, 0, 1, stride=1, stride_axis=0).astype(BF16)
    g_ref[...] = gain_ref[...]
    x_ref[0:144, :] = before_ref[16:160, :].astype(F32)
    x_ref[144:400, :] = k_ref[...].astype(F32)
    x_ref[400:416, :] = after_ref[288:304, :].astype(F32)
    total = jnp.zeros((392, 128), F32)
    for lag in range(FEAT):
        total = total + w_ref[1, lag : lag + 1, :] * x_ref[16 - lag : 408 - lag, :]
    kf_ref[...] = rounded(total)
    y_ref[0:16, :] = before_ref[0:16, :].astype(F32)
    y_ref[16:272, :] = q_ref[...].astype(F32)
    y_ref[272:416, :] = after_ref[0:144, :].astype(F32)
    total = jnp.zeros((392, 128), F32)
    for lag in range(FEAT):
        total = total + w_ref[0, lag : lag + 1, :] * y_ref[16 - lag : 408 - lag, :]
    qf = rounded(total)
    qf_ref[...] = qf[0:264]
    x_ref[0:256, :] = c_ref[...].astype(F32)
    x_ref[256:400, :] = after_ref[144:288, :].astype(F32)
    ce_ref[...] = x_ref[0:264, :]
    z_ref[0:384, :] = (x_ref[0:384, :] * qf[0:384]).astype(BF16)
    last = jnp.concatenate([x_ref[384:392, :] * qf[384:392], jnp.zeros((8, 128), F32)], axis=0)
    z_ref[384:400, :] = last.astype(BF16)
    z_ref[400:512, :] = jnp.zeros((112, 128), BF16)
    for b, part in enumerate(banded(bt_ref, z_ref)):
        dm_ref[128 * b : 128 * b + part.shape[0], :] = part


def finish(
    v_ref, before_ref, after_ref, w_ref, t_ref, kf_ref, qf_ref, ce_ref, dm_ref,
    o_ref, gq_ref, gk_ref, gv_ref,
    x_ref, z_ref, a_ref, b_ref, c_ref,
):
    x_ref[0:144, :] = before_ref[...].astype(F32)
    x_ref[144:400, :] = v_ref[...].astype(F32)
    x_ref[400:416, :] = after_ref[...].astype(F32)
    total = jnp.zeros((392, 128), F32)
    for lag in range(FEAT):
        total = total + w_ref[2, lag : lag + 1, :] * x_ref[16 - lag : 408 - lag, :]
    vf = rounded(total)
    kf = kf_ref[...]
    mixed = kf * vf
    z_ref[0:384, :] = mixed[0:384].astype(BF16)
    last = jnp.concatenate([mixed[384:392], jnp.zeros((8, 128), F32)], axis=0)
    z_ref[384:400, :] = last.astype(BF16)
    z_ref[400:512, :] = jnp.zeros((112, 128), BF16)
    for b, signal in enumerate(banded(t_ref, z_ref)):
        part = slice(128 * b, 128 * b + signal.shape[0])
        if b < 2:
            o_ref[part, :] = (qf_ref[part, :] * signal).astype(BF16)
        a_ref[part, :] = rounded(ce_ref[part, :] * signal)
    b_ref[...] = rounded(dm_ref[...] * vf[128:392])
    c_ref[...] = rounded(dm_ref[...] * kf[128:392])
    for i, (src, dst) in enumerate(((a_ref, gq_ref), (b_ref, gk_ref), (c_ref, gv_ref))):
        total = jnp.zeros((256, 128), F32)
        for lag in range(FEAT):
            total = total + w_ref[i, lag : lag + 1, :] * src[lag : lag + 256, :]
        dst[...] = total.astype(BF16)


def shape(dims, dtype=BF16):
    return jax.ShapeDtypeStruct(dims, dtype)


def call(body, outs, args, scratch=(), specs=None, flops=0, size=1 << 20, limit=8):
    single = not isinstance(outs, (list, tuple))
    return pl.pallas_call(
        body,
        out_shape=outs,
        in_specs=specs or [VM] * len(args),
        out_specs=VM if single else [VM] * len(outs),
        scratch_shapes=list(scratch),
        cost_estimate=pl.CostEstimate(flops=flops, bytes_accessed=size, transcendentals=0),
        compiler_params=pltpu.CompilerParams(vmem_limit_bytes=limit << 20),
    )(*args)


CTX = ("y_hi", "x", "core")
HEAD = ("y_lo", "z")


def neighbour(block, distance):
    n = lax.axis_size(CTX)
    return lax.ppermute(block, CTX, [(i, i + distance) for i in range(n) if 0 <= i + distance < n])


def per_device(q_att, k_att, v_att, norm_gain, hy_q, hy_k, feat_w, mr_filt, cotangent):
    info = jnp.stack([lax.axis_index("y_hi"), lax.axis_index("x"), lax.axis_index("core"), 0]).astype(jnp.int32)
    rows = lax.all_to_all(jnp.broadcast_to(q_att[None], (8, BLOCK, HD)), "x", 0, 0, tiled=True)
    both = jnp.concatenate([k_att, v_att], axis=0)
    came = [lax.ppermute(both, "y_hi", [(i, i + d) for i in range(4 - d)]) for d in (1, 2, 3)]
    own = jnp.stack([both] + came)
    other = lax.ppermute(own, "core", [(0, 1), (1, 0)])
    partial = call(
        attend,
        shape((8, 272, 128)),
        (info, rows, own, other),
        [
            pltpu.VMEM((4, 512, 128), BF16),
            pltpu.VMEM((4, 512, 256), BF16),
            pltpu.VMEM((8, 256, 256), F32),
            pltpu.VMEM((8, 256, 128), F32),
            pltpu.VMEM((8, 256, 512), F32),
            pltpu.VMEM((8, 256, 128), F32),
            pltpu.VMEM((256, 256), jnp.int32),
        ],
        specs=[SM, VM, VM, VM],
        flops=4 * 10**9,
        limit=24,
    )
    partial, hy_q, hy_k, cotangent = lax.optimization_barrier((partial, hy_q, hy_k, cotangent))
    parts = lax.all_to_all(partial, "x", 0, 0, tiled=True)
    before = neighbour(jnp.concatenate([hy_q[-16:], hy_k[-EXT:]], axis=0), 1)
    after = neighbour(jnp.concatenate([hy_q[:EXT], cotangent[:EXT], hy_k[:16]], axis=0), -1)
    parts, before, after = lax.optimization_barrier((parts, before, after))
    attended, sums = call(combine, [shape((256, 128)), shape((16, 8, 128), F32)], (parts,))
    sums, before, after = lax.optimization_barrier((sums, before, after))
    squares = lax.all_to_all(sums, HEAD, 0, 0, tiled=True)
    bands, kf, qf, ce, dm, gain = call(
        prepare,
        [shape((1024, 256)), shape((392, 128), F32), shape((264, 128), F32), shape((264, 128), F32), shape((264, 128), F32), shape((1, 128), F32)],
        (hy_q, hy_k, cotangent, before, after, feat_w, mr_filt, norm_gain[None]),
        [pltpu.VMEM((1024, 256), BF16), pltpu.VMEM((416, 128), F32), pltpu.VMEM((416, 128), F32), pltpu.VMEM((512, 128), BF16)],
        flops=10**9,
    )
    squares, bands, kf, qf, ce, dm, gain = lax.optimization_barrier((squares, bands, kf, qf, ce, dm, gain))
    value, end, begin = call(
        normalize, [shape((256, 128)), shape((EXT, 128)), shape((16, 128))], (attended, squares, gain)
    )
    v_before = neighbour(end, 1)
    v_after = neighbour(begin, -1)
    return tuple(
        call(
            finish,
            [shape((256, 128))] * 4,
            (value, v_before, v_after, feat_w, bands, kf, qf, ce, dm),
            [pltpu.VMEM((416, 128), F32), pltpu.VMEM((512, 128), BF16)] + [pltpu.VMEM((264, 128), F32)] * 3,
        )
    )


def solution(mesh):
    fine = Mesh(mesh.devices.reshape(4, 8, 2, 2, 8), CTX + HEAD)
    tokens = P(CTX, HEAD)
    placed = (tokens, tokens, tokens, P(HEAD), tokens, tokens, P(None, None, HEAD), P(None, HEAD), tokens)
    return jax.shard_map(per_device, mesh=fine, in_specs=placed, out_specs=(tokens,) * 4, check_vma=False)
```

```python
import functools
import math

import jax
import jax.numpy as jnp
from jax import lax
from jax.experimental import pallas as pl
from jax.experimental.pallas import tpu as pltpu
from jax.sharding import Mesh, PartitionSpec as P


HD = 128
GROUP_CH = 16
FEAT = 7
BLOCK = 256
NEGATIVE = -1e30
EPSILON = 1e-06
LOG2E = 1.4426950408889634
FACTOR = LOG2E / math.sqrt(HD)
F32 = jnp.float32
BF16 = jnp.bfloat16


VM = pl.BlockSpec(memory_space=pltpu.VMEM)
SM = pl.BlockSpec(memory_space=pltpu.SMEM)


def rounded(x):
    return x.astype(BF16).astype(F32)


def dot(a, b, dims):
    return lax.dot_general(a, b, (dims, ((), ())), preferred_element_type=F32)


def to_rows(x):
    i = lax.broadcasted_iota(jnp.int32, (128, 128), 0)
    j = lax.broadcasted_iota(jnp.int32, (128, 128), 1)
    return jnp.sum(jnp.where(i == j, x, 0.0), axis=0, keepdims=True)


def stacked(rows, height):
    at = lax.broadcasted_iota(jnp.int32, (height, 128), 0)
    out = jnp.zeros((height, 128), F32)
    for i, row in enumerate(rows):
        out = jnp.where(at == i, row, out)
    return out


def attend(info, q_ref, own_ref, oth_ref, o_ref, k_ref, v_ref, acc_ref, m_ref, s_ref, t_ref, d_ref):
    plane, column, core = info[0], info[1], info[2]

    def fill(p, c):
        for half, src in ((0, own_ref), (1, oth_ref)):
            keys = src[p, 0:256, :]
            k_ref[p, 256 * half : 256 * half + 256, :] = keys
            v_ref[p, 256 * half : 256 * half + 256, :] = jnp.concatenate(
                [src[p, 256:512, :], jnp.ones((256, 128), BF16)], axis=1
            )
        return c

    lax.fori_loop(0, plane + 1, fill, 0)

    def split(b, c):
        acc_ref[b] = jnp.zeros((256, 256), F32)
        m_ref[b] = jnp.full((256, 128), NEGATIVE, F32)
        return c

    lax.fori_loop(0, 8, split, 0)

    i = lax.broadcasted_iota(jnp.int32, (256, 256), 0)
    j = lax.broadcasted_iota(jnp.int32, (256, 256), 1)
    d_ref[...] = j - i

    def scores(n, b, p, masked):
        s = dot(q_ref[b], k_ref[p], ((1,), (1,))) * FACTOR
        if masked:
            bound = jnp.where(b > column, 512, jnp.where(b == column, 0, -512))
            seen = jnp.where(b > column, 1, jnp.where(b == column, core, 0))
            s = jnp.concatenate(
                [
                    jnp.where(d_ref[...] <= bound, s[:, 0:256], NEGATIVE),
                    jnp.where(jnp.full((256, 256), seen, jnp.int32) == 1, s[:, 256:512], NEGATIVE),
                ],
                axis=1,
            )
        s_ref[n] = s
        t_ref[n] = jnp.broadcast_to(jnp.max(s, axis=1, keepdims=True), (256, 128))

    def update(n, b, p):
        old = m_ref[b]
        new = jnp.maximum(old, rounded(t_ref[n]))
        m_ref[b] = new
        scale = jnp.exp2(old - new)
        e = jnp.concatenate([jnp.exp2(s_ref[n, :, 128 * k : 128 * k + 128] - new) for k in range(4)], axis=1)
        add = dot(e.astype(BF16), v_ref[p], ((1,), (0,)))
        acc_ref[b, :, 0:128] = acc_ref[b, :, 0:128] * scale + add[:, 0:128]
        acc_ref[b, :, 128:256] = acc_ref[b, :, 128:256] * scale + add[:, 128:256]

    def some(first, p, masked):
        for n in range(8):
            scores(n, first + n, p, masked)
            if n:
                update(n - 1, first + n - 1, p)
        update(8 - 1, first + 8 - 1, p)

    def same(g, c):
        @pl.when(8 * (g + 1) > column)
        def _():
            some(8 * g, 0, True)

        return c

    lax.fori_loop(0, 8 // 8, same, 0)

    def past(g, c):
        some(8 * lax.rem(g, 8 // 8), 1 + lax.div(g, 8 // 8), False)
        return c

    lax.fori_loop(0, plane * (8 // 8), past, 0)

    def emit(b, c):
        o_ref[b, 0:256, :] = acc_ref[b, :, 0:128].astype(BF16)
        tops, high, low = [], [], []
        for h in range(2):
            part = slice(128 * h, 128 * h + 128)
            tops.append(to_rows(m_ref[b, part, :]))
            mass = to_rows(acc_ref[b, part, 128:256])
            upper = rounded(mass)
            high.append(upper)
            low.append(mass - upper)
        o_ref[b, 256:272, :] = stacked(tops + high + low, 16).astype(BF16)
        return c

    lax.fori_loop(0, 8, emit, 0)


def combine(msg_ref, a_ref, s_ref):
    copies = s_ref.shape[0]
    n = msg_ref.shape[0]
    stats = [msg_ref[i, 256:272, :].astype(F32) for i in range(n)]
    sums = []
    for h in range(2):
        tops = [s[h : h + 1] for s in stats]
        totals = [s[2 + h : 3 + h] + s[4 + h : 5 + h] for s in stats]
        top = functools.reduce(jnp.maximum, tops)
        weights = [jnp.exp2(t - top) for t in tops]
        total = sum(w * t for w, t in zip(weights, totals))
        shares = jnp.transpose(stacked([w / total for w in weights], 128))
        out = jnp.zeros((128, 128), F32)
        for i in range(n):
            out = out + shares[:, i : i + 1] * msg_ref[i, 128 * h : 128 * h + 128, :].astype(F32)
        out = out.astype(BF16)
        a_ref[128 * h : 128 * h + 128, :] = out
        square = out.astype(F32) * out.astype(F32)
        upper = square.astype(BF16)
        lower = (square - upper.astype(F32)).astype(BF16)
        ones = jnp.ones((8, 128), BF16)
        sums.append((dot(ones, upper, ((1,), (1,))) + dot(ones, lower, ((1,), (1,))))[0:1])
    both = stacked(sums, 8)
    for i in range(copies):
        s_ref[i] = both


def normalize(a_ref, s_ref, g_ref, q_ref, k_ref, c_ref, v_ref, end_ref, begin_ref):
    n = s_ref.shape[0]
    total = functools.reduce(jnp.add, [s_ref[i] for i in range(n)])
    scale = lax.rsqrt(total * (1.0 / (n * 128)) + EPSILON)
    column = jnp.transpose(jnp.concatenate([scale, jnp.zeros((120, 128), F32)], axis=0))
    for h in range(2):
        part = slice(128 * h, 128 * h + 128)
        v_ref[part, :] = (a_ref[part, :].astype(F32) * column[:, h : h + 1] * g_ref[...]).astype(BF16)
    end_ref[0:144, :] = v_ref[112:256, :]
    end_ref[144:160, :] = q_ref[240:256, :]
    end_ref[160:304, :] = k_ref[112:256, :]
    begin_ref[0:16, :] = v_ref[0:16, :]
    begin_ref[16:160, :] = q_ref[0:144, :]
    begin_ref[160:304, :] = c_ref[0:144, :]
    begin_ref[304:320, :] = k_ref[0:16, :]


def picked(stack, rows):
    lane = lax.broadcasted_iota(jnp.int32, (rows, 128), 1) // GROUP_CH
    out = stack[0:rows]
    for g in range(1, 8):
        out = jnp.where(lane == g, stack[g * rows : (g + 1) * rows], out)
    return out


def banded(bands, data_ref):
    out = []
    for b in range(2):
        out.append(picked(dot(bands[...], data_ref[128 * b : 128 * b + 256, :], ((1,), (0,))), 128))
    tail = jnp.concatenate([bands[128 * g : 128 * g + 16, :] for g in range(8)], axis=0)
    out.append(picked(dot(tail, data_ref[256:512, :], ((1,), (0,))), 16)[0:8])
    return out


def build(f_ref, gain_ref, t_ref, bt_ref, g_ref):
    g_ref[...] = gain_ref[...]
    i = lax.broadcasted_iota(jnp.int32, (128, 128), 0)
    j = lax.broadcasted_iota(jnp.int32, (128, 128), 1)
    taps = f_ref[...].astype(BF16)
    front = dot(taps, (i + j == 128).astype(BF16), ((0,), (0,)))
    first = jnp.where(
        lax.broadcasted_iota(jnp.int32, (8, 128), 1) == 0, dot(taps, (i == 0).astype(BF16), ((0,), (0,))), 0.0
    )
    back = dot(taps, (i == j).astype(BF16), ((0,), (0,)))
    front = jnp.concatenate([front, first], axis=1)
    back = jnp.concatenate([back, jnp.zeros((8, 128), F32)], axis=1)
    for g in range(8):
        row = jnp.broadcast_to(front[g : g + 1, :], (128, 256))
        t_ref[128 * g : 128 * g + 128, :] = pltpu.roll(row, 0, 1, stride=1, stride_axis=0).astype(BF16)
        row = jnp.broadcast_to(back[g : g + 1, :], (128, 256))
        bt_ref[128 * g : 128 * g + 128, :] = pltpu.roll(row, 0, 1, stride=1, stride_axis=0).astype(BF16)


def featurized(x_ref, w_ref, index):
    total = jnp.zeros((392, 128), F32)
    for lag in range(FEAT):
        total = total + w_ref[index, lag : lag + 1, :] * x_ref[16 - lag : 408 - lag, :]
    return rounded(total)


def put(z_ref, x):
    z_ref[0:384, :] = x[0:384].astype(BF16)
    z_ref[384:400, :] = jnp.concatenate([x[384:392], jnp.zeros((8, 128), F32)], axis=0).astype(BF16)
    z_ref[400:512, :] = jnp.zeros((112, 128), BF16)


def finish(
    v_ref, q_ref, k_ref, c_ref, before_ref, after_ref, w_ref, t_ref, bt_ref,
    o_ref, gq_ref, gk_ref, gv_ref,
    x_ref, y_ref, s_ref, e_ref, m_ref, n_ref, a_ref, b_ref, d_ref, h_ref,
):
    y_ref[0:16, :] = before_ref[144:160, :].astype(F32)
    y_ref[16:272, :] = q_ref[...].astype(F32)
    y_ref[272:416, :] = after_ref[16:160, :].astype(F32)
    qf = featurized(y_ref, w_ref, 0)
    e_ref[0:256, :] = c_ref[...].astype(F32)
    e_ref[256:400, :] = after_ref[160:304, :].astype(F32)
    put(n_ref, e_ref[0:392, :] * qf)
    x_ref[0:144, :] = before_ref[160:304, :].astype(F32)
    x_ref[144:400, :] = k_ref[...].astype(F32)
    x_ref[400:416, :] = after_ref[304:320, :].astype(F32)
    kf = featurized(x_ref, w_ref, 1)
    s_ref[0:144, :] = before_ref[0:144, :].astype(F32)
    s_ref[144:400, :] = v_ref[...].astype(F32)
    s_ref[400:416, :] = after_ref[0:16, :].astype(F32)
    vf = featurized(s_ref, w_ref, 2)
    put(m_ref, kf * vf)
    for b, back in enumerate(banded(bt_ref, n_ref)):
        d_ref[128 * b : 128 * b + back.shape[0], :] = back
    for b, signal in enumerate(banded(t_ref, m_ref)):
        part = slice(128 * b, 128 * b + signal.shape[0])
        if b < 2:
            o_ref[part, :] = (qf[part] * signal).astype(BF16)
        a_ref[part, :] = rounded(e_ref[part, :] * signal)
    b_ref[...] = rounded(d_ref[...] * vf[128:392])
    h_ref[...] = rounded(d_ref[...] * kf[128:392])
    for i, (src, dst) in enumerate(((a_ref, gq_ref), (b_ref, gk_ref), (h_ref, gv_ref))):
        total = jnp.zeros((256, 128), F32)
        for lag in range(FEAT):
            total = total + w_ref[i, lag : lag + 1, :] * src[lag : lag + 256, :]
        dst[...] = total.astype(BF16)


def shape(dims, dtype=BF16):
    return jax.ShapeDtypeStruct(dims, dtype)


def call(body, outs, args, scratch=(), specs=None, flops=0, size=1 << 20, limit=8):
    single = not isinstance(outs, (list, tuple))
    return pl.pallas_call(
        body,
        out_shape=outs,
        in_specs=specs or [VM] * len(args),
        out_specs=VM if single else [VM] * len(outs),
        scratch_shapes=list(scratch),
        cost_estimate=pl.CostEstimate(flops=flops, bytes_accessed=size, transcendentals=0),
        compiler_params=pltpu.CompilerParams(vmem_limit_bytes=limit << 20),
    )(*args)


CTX = ("y_hi", "x", "core")
HEAD = ("y_lo", "z")


def neighbour(block, distance):
    n = lax.axis_size(CTX)
    return lax.ppermute(block, CTX, [(i, i + distance) for i in range(n) if 0 <= i + distance < n])


def per_device(q_att, k_att, v_att, norm_gain, hy_q, hy_k, feat_w, mr_filt, cotangent):
    info = jnp.stack([lax.axis_index("y_hi"), lax.axis_index("x"), lax.axis_index("core"), 0]).astype(jnp.int32)
    both = jnp.concatenate([k_att, v_att], axis=0)
    came = []
    for d in (1, 2, 3):
        came.append(lax.ppermute(both, "y_hi", [(i, i + d) for i in range(4 - d)]))
    rows = lax.all_to_all(jnp.broadcast_to(q_att[None], (8, BLOCK, HD)), "x", 0, 0, tiled=True)
    own = jnp.stack([both] + came)
    other = lax.ppermute(own, "core", [(0, 1), (1, 0)])
    bands, back_bands, gain = call(
        build, [shape((1024, 256))] * 2 + [shape((1, 128), F32)], (mr_filt, norm_gain[None]), flops=4 * 10**8
    )
    info, rows, own, other, bands, back_bands, gain = lax.optimization_barrier(
        (info, rows, own, other, bands, back_bands, gain)
    )
    partial = call(
        attend,
        shape((8, 272, 128)),
        (info, rows, own, other),
        [
            pltpu.VMEM((4, 512, 128), BF16),
            pltpu.VMEM((4, 512, 256), BF16),
            pltpu.VMEM((8, 256, 256), F32),
            pltpu.VMEM((8, 256, 128), F32),
            pltpu.VMEM((8, 256, 512), F32),
            pltpu.VMEM((8, 256, 128), F32),
            pltpu.VMEM((256, 256), jnp.int32),
        ],
        specs=[SM, VM, VM, VM],
        flops=4 * 10**9,
        limit=24,
    )
    parts = lax.all_to_all(partial, "x", 0, 0, tiled=True)
    attended, sums = call(combine, [shape((256, 128)), shape((16, 8, 128), F32)], (parts,))
    squares = lax.all_to_all(sums, HEAD, 0, 0, tiled=True)
    value, end, begin = call(
        normalize,
        [shape((256, 128)), shape((304, 128)), shape((320, 128))],
        (attended, squares, gain, hy_q, hy_k, cotangent),
    )
    before = neighbour(end, 1)
    after = neighbour(begin, -1)
    tall = pltpu.VMEM((416, 128), F32)
    return tuple(
        call(
            finish,
            [shape((256, 128))] * 4,
            (value, hy_q, hy_k, cotangent, before, after, feat_w, bands, back_bands),
            [tall] * 4 + [pltpu.VMEM((512, 128), BF16)] * 2 + [pltpu.VMEM((264, 128), F32)] * 4,
        )
    )


def solution(mesh):
    fine = Mesh(mesh.devices.reshape(4, 8, 2, 2, 8), CTX + HEAD)
    tokens = P(CTX, HEAD)
    placed = (tokens, tokens, tokens, P(HEAD), tokens, tokens, P(None, None, HEAD), P(None, HEAD), tokens)
    return jax.shard_map(per_device, mesh=fine, in_specs=placed, out_specs=(tokens,) * 4, check_vma=False)
```

```python
import functools
import math

import jax
import jax.numpy as jnp
from jax import lax
from jax.experimental import pallas as pl
from jax.experimental.pallas import tpu as pltpu
from jax.sharding import Mesh, PartitionSpec as P


HD = 128
GROUP_CH = 16
FEAT = 7
BLOCK = 256
NEGATIVE = -1e30
EPSILON = 1e-06
LOG2E = 1.4426950408889634
FACTOR = LOG2E / math.sqrt(HD)
F32 = jnp.float32
BF16 = jnp.bfloat16


VM = pl.BlockSpec(memory_space=pltpu.VMEM)
SM = pl.BlockSpec(memory_space=pltpu.SMEM)


def rounded(x):
    return x.astype(BF16).astype(F32)


def dot(a, b, dims):
    return lax.dot_general(a, b, (dims, ((), ())), preferred_element_type=F32)


def to_rows(x):
    i = lax.broadcasted_iota(jnp.int32, (128, 128), 0)
    j = lax.broadcasted_iota(jnp.int32, (128, 128), 1)
    return jnp.sum(jnp.where(i == j, x, 0.0), axis=0, keepdims=True)


def stacked(rows, height):
    at = lax.broadcasted_iota(jnp.int32, (height, 128), 0)
    out = jnp.zeros((height, 128), F32)
    for i, row in enumerate(rows):
        out = jnp.where(at == i, row, out)
    return out


def attend(info, q_ref, own_ref, oth_ref, o_ref, k_ref, v_ref, acc_ref, m_ref, s_ref, t_ref, d_ref):
    plane, column, core = info[0], info[1], info[2]

    def fill(p, c):
        for half, src in ((0, own_ref), (1, oth_ref)):
            keys = src[p, 0:256, :]
            k_ref[p, 256 * half : 256 * half + 256, :] = keys
            v_ref[p, 256 * half : 256 * half + 256, :] = jnp.concatenate(
                [src[p, 256:512, :], jnp.ones((256, 128), BF16)], axis=1
            )
        return c

    lax.fori_loop(0, plane + 1, fill, 0)

    def split(b, c):
        acc_ref[b] = jnp.zeros((256, 256), F32)
        m_ref[b] = jnp.full((256, 128), NEGATIVE, F32)
        return c

    lax.fori_loop(0, 8, split, 0)

    i = lax.broadcasted_iota(jnp.int32, (256, 256), 0)
    j = lax.broadcasted_iota(jnp.int32, (256, 256), 1)
    d_ref[...] = j - i

    def scores(n, b, p, masked):
        s = dot(q_ref[b], k_ref[p], ((1,), (1,))) * FACTOR
        if masked:
            bound = jnp.where(b > column, 512, jnp.where(b == column, 0, -512))
            seen = jnp.where(b > column, 1, jnp.where(b == column, core, 0))
            s = jnp.concatenate(
                [
                    jnp.where(d_ref[...] <= bound, s[:, 0:256], NEGATIVE),
                    jnp.where(jnp.full((256, 256), seen, jnp.int32) == 1, s[:, 256:512], NEGATIVE),
                ],
                axis=1,
            )
        s_ref[n] = s
        t_ref[n] = jnp.broadcast_to(jnp.max(s, axis=1, keepdims=True), (256, 128))

    def update(n, b, p):
        old = m_ref[b]
        new = jnp.maximum(old, rounded(t_ref[n]))
        m_ref[b] = new
        scale = jnp.exp2(old - new)
        e = jnp.concatenate([jnp.exp2(s_ref[n, :, 128 * k : 128 * k + 128] - new) for k in range(4)], axis=1)
        add = dot(e.astype(BF16), v_ref[p], ((1,), (0,)))
        acc_ref[b, :, 0:128] = acc_ref[b, :, 0:128] * scale + add[:, 0:128]
        acc_ref[b, :, 128:256] = acc_ref[b, :, 128:256] * scale + add[:, 128:256]

    def some(first, p, masked):
        for n in range(8):
            scores(n, first + n, p, masked)
            if n:
                update(n - 1, first + n - 1, p)
        update(8 - 1, first + 8 - 1, p)

    def same(g, c):
        @pl.when(8 * (g + 1) > column)
        def _():
            some(8 * g, 0, True)

        return c

    lax.fori_loop(0, 8 // 8, same, 0)

    def past(g, c):
        some(8 * lax.rem(g, 8 // 8), 1 + lax.div(g, 8 // 8), False)
        return c

    lax.fori_loop(0, plane * (8 // 8), past, 0)

    def emit(b, c):
        o_ref[b, 0:256, :] = acc_ref[b, :, 0:128].astype(BF16)
        tops, high, low = [], [], []
        for h in range(2):
            part = slice(128 * h, 128 * h + 128)
            tops.append(to_rows(m_ref[b, part, :]))
            mass = to_rows(acc_ref[b, part, 128:256])
            upper = rounded(mass)
            high.append(upper)
            low.append(mass - upper)
        o_ref[b, 256:264, :] = stacked(tops + high + low, 8).astype(BF16)
        return c

    lax.fori_loop(0, 8, emit, 0)


def combine(msg_ref, a_ref, s_ref):
    copies = s_ref.shape[0]
    n = msg_ref.shape[0]
    stats = [msg_ref[i, 256:264, :].astype(F32) for i in range(n)]
    sums = []
    for h in range(2):
        tops = [s[h : h + 1] for s in stats]
        totals = [s[2 + h : 3 + h] + s[4 + h : 5 + h] for s in stats]
        top = functools.reduce(jnp.maximum, tops)
        weights = [jnp.exp2(t - top) for t in tops]
        total = sum(w * t for w, t in zip(weights, totals))
        shares = jnp.transpose(stacked([w / total for w in weights], 128))
        out = jnp.zeros((128, 128), F32)
        for i in range(n):
            out = out + shares[:, i : i + 1] * msg_ref[i, 128 * h : 128 * h + 128, :].astype(F32)
        out = out.astype(BF16)
        a_ref[128 * h : 128 * h + 128, :] = out
        square = out.astype(F32) * out.astype(F32)
        upper = square.astype(BF16)
        lower = (square - upper.astype(F32)).astype(BF16)
        ones = jnp.ones((8, 128), BF16)
        sums.append((dot(ones, upper, ((1,), (1,))) + dot(ones, lower, ((1,), (1,))))[0:1])
    both = stacked(sums, 8)
    for i in range(copies):
        s_ref[i] = both


def normalize(a_ref, s_ref, g_ref, q_ref, k_ref, c_ref, v_ref, end_ref, begin_ref):
    n = s_ref.shape[0]
    total = functools.reduce(jnp.add, [s_ref[i] for i in range(n)])
    scale = lax.rsqrt(total * (1.0 / (n * 128)) + EPSILON)
    column = jnp.transpose(jnp.concatenate([scale, jnp.zeros((120, 128), F32)], axis=0))
    for h in range(2):
        part = slice(128 * h, 128 * h + 128)
        v_ref[part, :] = (a_ref[part, :].astype(F32) * column[:, h : h + 1] * g_ref[...]).astype(BF16)
    end_ref[0:144, :] = v_ref[112:256, :]
    end_ref[144:160, :] = q_ref[240:256, :]
    end_ref[160:304, :] = k_ref[112:256, :]
    begin_ref[0:16, :] = v_ref[0:16, :]
    begin_ref[16:160, :] = q_ref[0:144, :]
    begin_ref[160:304, :] = c_ref[0:144, :]
    begin_ref[304:320, :] = k_ref[0:16, :]


def picked(stack, rows):
    lane = lax.broadcasted_iota(jnp.int32, (rows, 128), 1) // GROUP_CH
    out = stack[0:rows]
    for g in range(1, 8):
        out = jnp.where(lane == g, stack[g * rows : (g + 1) * rows], out)
    return out


def banded(bands, data_ref):
    out = []
    for b in range(2):
        out.append(picked(dot(bands[...], data_ref[128 * b : 128 * b + 256, :], ((1,), (0,))), 128))
    tail = jnp.concatenate([bands[128 * g : 128 * g + 16, :] for g in range(8)], axis=0)
    out.append(picked(dot(tail, data_ref[256:512, :], ((1,), (0,))), 16)[0:8])
    return out


def build(f_ref, gain_ref, t_ref, bt_ref, g_ref):
    g_ref[...] = gain_ref[...]
    i = lax.broadcasted_iota(jnp.int32, (128, 128), 0)
    j = lax.broadcasted_iota(jnp.int32, (128, 128), 1)
    taps = f_ref[...].astype(BF16)
    front = dot(taps, (i + j == 128).astype(BF16), ((0,), (0,)))
    first = jnp.where(
        lax.broadcasted_iota(jnp.int32, (8, 128), 1) == 0, dot(taps, (i == 0).astype(BF16), ((0,), (0,))), 0.0
    )
    back = dot(taps, (i == j).astype(BF16), ((0,), (0,)))
    front = jnp.concatenate([front, first], axis=1)
    back = jnp.concatenate([back, jnp.zeros((8, 128), F32)], axis=1)
    for g in range(8):
        row = jnp.broadcast_to(front[g : g + 1, :], (128, 256))
        t_ref[128 * g : 128 * g + 128, :] = pltpu.roll(row, 0, 1, stride=1, stride_axis=0).astype(BF16)
        row = jnp.broadcast_to(back[g : g + 1, :], (128, 256))
        bt_ref[128 * g : 128 * g + 128, :] = pltpu.roll(row, 0, 1, stride=1, stride_axis=0).astype(BF16)


def featurized(x_ref, w_ref, index):
    total = jnp.zeros((392, 128), F32)
    for lag in range(FEAT):
        total = total + w_ref[index, lag : lag + 1, :] * x_ref[16 - lag : 408 - lag, :]
    return rounded(total)


def put(z_ref, x):
    z_ref[0:384, :] = x[0:384].astype(BF16)
    z_ref[384:400, :] = jnp.concatenate([x[384:392], jnp.zeros((8, 128), F32)], axis=0).astype(BF16)
    z_ref[400:512, :] = jnp.zeros((112, 128), BF16)


def finish(
    v_ref, q_ref, k_ref, c_ref, before_ref, after_ref, w_ref, t_ref, bt_ref,
    o_ref, gq_ref, gk_ref, gv_ref,
    x_ref, y_ref, s_ref, e_ref, m_ref, n_ref, a_ref, b_ref, d_ref, h_ref,
):
    y_ref[0:16, :] = before_ref[144:160, :].astype(F32)
    y_ref[16:272, :] = q_ref[...].astype(F32)
    y_ref[272:416, :] = after_ref[16:160, :].astype(F32)
    qf = featurized(y_ref, w_ref, 0)
    e_ref[0:256, :] = c_ref[...].astype(F32)
    e_ref[256:400, :] = after_ref[160:304, :].astype(F32)
    put(n_ref, e_ref[0:392, :] * qf)
    x_ref[0:144, :] = before_ref[160:304, :].astype(F32)
    x_ref[144:400, :] = k_ref[...].astype(F32)
    x_ref[400:416, :] = after_ref[304:320, :].astype(F32)
    kf = featurized(x_ref, w_ref, 1)
    s_ref[0:144, :] = before_ref[0:144, :].astype(F32)
    s_ref[144:400, :] = v_ref[...].astype(F32)
    s_ref[400:416, :] = after_ref[0:16, :].astype(F32)
    vf = featurized(s_ref, w_ref, 2)
    put(m_ref, kf * vf)
    for b, back in enumerate(banded(bt_ref, n_ref)):
        d_ref[128 * b : 128 * b + back.shape[0], :] = back
    for b, signal in enumerate(banded(t_ref, m_ref)):
        part = slice(128 * b, 128 * b + signal.shape[0])
        if b < 2:
            o_ref[part, :] = (qf[part] * signal).astype(BF16)
        a_ref[part, :] = rounded(e_ref[part, :] * signal)
    b_ref[...] = rounded(d_ref[...] * vf[128:392])
    h_ref[...] = rounded(d_ref[...] * kf[128:392])
    for i, (src, dst) in enumerate(((a_ref, gq_ref), (b_ref, gk_ref), (h_ref, gv_ref))):
        total = jnp.zeros((256, 128), F32)
        for lag in range(FEAT):
            total = total + w_ref[i, lag : lag + 1, :] * src[lag : lag + 256, :]
        dst[...] = total.astype(BF16)


def shape(dims, dtype=BF16):
    return jax.ShapeDtypeStruct(dims, dtype)


def call(body, outs, args, scratch=(), specs=None, flops=0, size=1 << 20, limit=8):
    single = not isinstance(outs, (list, tuple))
    return pl.pallas_call(
        body,
        out_shape=outs,
        in_specs=specs or [VM] * len(args),
        out_specs=VM if single else [VM] * len(outs),
        scratch_shapes=list(scratch),
        cost_estimate=pl.CostEstimate(flops=flops, bytes_accessed=size, transcendentals=0),
        compiler_params=pltpu.CompilerParams(vmem_limit_bytes=limit << 20),
    )(*args)


CTX = ("y_hi", "x", "core")
HEAD = ("y_lo", "z")


def neighbour(block, distance):
    n = lax.axis_size(CTX)
    return lax.ppermute(block, CTX, [(i, i + distance) for i in range(n) if 0 <= i + distance < n])


def per_device(q_att, k_att, v_att, norm_gain, hy_q, hy_k, feat_w, mr_filt, cotangent):
    info = jnp.stack([lax.axis_index("y_hi"), lax.axis_index("x"), lax.axis_index("core"), 0]).astype(jnp.int32)
    both = jnp.concatenate([k_att, v_att], axis=0)
    came = []
    for d in (1, 2, 3):
        came.append(lax.ppermute(both, "y_hi", [(i, i + d) for i in range(4 - d)]))
    rows = lax.all_to_all(jnp.broadcast_to(q_att[None], (8, BLOCK, HD)), "x", 0, 0, tiled=True)
    own = jnp.stack([both] + came)
    other = lax.ppermute(own, "core", [(0, 1), (1, 0)])
    bands, back_bands, gain = call(
        build, [shape((1024, 256))] * 2 + [shape((1, 128), F32)], (mr_filt, norm_gain[None]), flops=4 * 10**8
    )
    info, rows, own, other, bands, back_bands, gain = lax.optimization_barrier(
        (info, rows, own, other, bands, back_bands, gain)
    )
    partial = call(
        attend,
        shape((8, 264, 128)),
        (info, rows, own, other),
        [
            pltpu.VMEM((4, 512, 128), BF16),
            pltpu.VMEM((4, 512, 256), BF16),
            pltpu.VMEM((8, 256, 256), F32),
            pltpu.VMEM((8, 256, 128), F32),
            pltpu.VMEM((8, 256, 512), F32),
            pltpu.VMEM((8, 256, 128), F32),
            pltpu.VMEM((256, 256), jnp.int32),
        ],
        specs=[SM, VM, VM, VM],
        flops=4 * 10**9,
        limit=24,
    )
    parts = lax.all_to_all(partial, "x", 0, 0, tiled=True)
    attended, sums = call(combine, [shape((256, 128)), shape((16, 8, 128), F32)], (parts,))
    squares = lax.all_to_all(sums, HEAD, 0, 0, tiled=True)
    value, end, begin = call(
        normalize,
        [shape((256, 128)), shape((304, 128)), shape((320, 128))],
        (attended, squares, gain, hy_q, hy_k, cotangent),
    )
    before = neighbour(end, 1)
    after = neighbour(begin, -1)
    tall = pltpu.VMEM((416, 128), F32)
    return tuple(
        call(
            finish,
            [shape((256, 128))] * 4,
            (value, hy_q, hy_k, cotangent, before, after, feat_w, bands, back_bands),
            [tall] * 4 + [pltpu.VMEM((512, 128), BF16)] * 2 + [pltpu.VMEM((264, 128), F32)] * 4,
        )
    )


def solution(mesh):
    fine = Mesh(mesh.devices.reshape(4, 8, 2, 2, 8), CTX + HEAD)
    tokens = P(CTX, HEAD)
    placed = (tokens, tokens, tokens, P(HEAD), tokens, tokens, P(None, None, HEAD), P(None, HEAD), tokens)
    return jax.shard_map(per_device, mesh=fine, in_specs=placed, out_specs=(tokens,) * 4, check_vma=False)
```

```python
import functools
import math

import jax
import jax.numpy as jnp
from jax import lax
from jax.experimental import pallas as pl
from jax.experimental.pallas import tpu as pltpu
from jax.sharding import Mesh, PartitionSpec as P


HD = 128
GROUP_CH = 16
FEAT = 7
BLOCK = 256
NEGATIVE = -1e30
EPSILON = 1e-06
LOG2E = 1.4426950408889634
FACTOR = LOG2E / math.sqrt(HD)
F32 = jnp.float32
BF16 = jnp.bfloat16


VM = pl.BlockSpec(memory_space=pltpu.VMEM)
SM = pl.BlockSpec(memory_space=pltpu.SMEM)


def rounded(x):
    return x.astype(BF16).astype(F32)


def dot(a, b, dims):
    return lax.dot_general(a, b, (dims, ((), ())), preferred_element_type=F32)


def to_rows(x):
    i = lax.broadcasted_iota(jnp.int32, (128, 128), 0)
    j = lax.broadcasted_iota(jnp.int32, (128, 128), 1)
    return jnp.sum(jnp.where(i == j, x, 0.0), axis=0, keepdims=True)


def stacked(rows, height):
    at = lax.broadcasted_iota(jnp.int32, (height, 128), 0)
    out = jnp.zeros((height, 128), F32)
    for i, row in enumerate(rows):
        out = jnp.where(at == i, row, out)
    return out


def attend(info, q_ref, own_ref, oth_ref, o_ref, k_ref, v_ref, acc_ref, m_ref, s_ref, t_ref, d_ref):
    plane, column, core = info[0], info[1], info[2]

    def fill(p, c):
        for half, src in ((0, own_ref), (1, oth_ref)):
            keys = src[p, 0:256, :]
            k_ref[p, 256 * half : 256 * half + 256, :] = keys
            v_ref[p, 256 * half : 256 * half + 256, :] = jnp.concatenate(
                [src[p, 256:512, :], jnp.ones((256, 128), BF16)], axis=1
            )
        return c

    lax.fori_loop(0, plane + 1, fill, 0)

    i = lax.broadcasted_iota(jnp.int32, (256, 256), 0)
    j = lax.broadcasted_iota(jnp.int32, (256, 256), 1)
    d_ref[...] = j - i

    def scores(n, b, p, masked):
        s = dot(q_ref[b], k_ref[p], ((1,), (1,))) * FACTOR
        if masked:
            bound = jnp.where(b > column, 512, jnp.where(b == column, 0, -512))
            seen = jnp.where(b > column, 1, jnp.where(b == column, core, 0))
            s = jnp.concatenate(
                [
                    jnp.where(d_ref[...] <= bound, s[:, 0:256], NEGATIVE),
                    jnp.where(jnp.full((256, 256), seen, jnp.int32) == 1, s[:, 256:512], NEGATIVE),
                ],
                axis=1,
            )
        s_ref[n] = s
        t_ref[n] = jnp.broadcast_to(jnp.max(s, axis=1, keepdims=True), (256, 128))

    def update(n, b, p, first):
        if first:
            new = jnp.maximum(rounded(t_ref[n]), NEGATIVE)
        else:
            old = m_ref[b]
            new = jnp.maximum(old, rounded(t_ref[n]))
            scale = jnp.exp2(old - new)
        m_ref[b] = new
        e = jnp.concatenate([jnp.exp2(s_ref[n, :, 128 * k : 128 * k + 128] - new) for k in range(4)], axis=1)
        add = dot(e.astype(BF16), v_ref[p], ((1,), (0,)))
        if first:
            acc_ref[b] = add
        else:
            acc_ref[b, :, 0:128] = acc_ref[b, :, 0:128] * scale + add[:, 0:128]
            acc_ref[b, :, 128:256] = acc_ref[b, :, 128:256] * scale + add[:, 128:256]

    def every(p, first):
        for n in range(8):
            scores(n, n, p, first)
            if n:
                update(n - 1, n - 1, p, first)
        update(7, 7, p, first)

    every(0, True)

    def past(p, c):
        every(p, False)
        return c

    lax.fori_loop(1, plane + 1, past, 0)

    def emit(b, c):
        o_ref[b, 0:256, :] = acc_ref[b, :, 0:128].astype(BF16)
        tops, high, low = [], [], []
        for h in range(2):
            part = slice(128 * h, 128 * h + 128)
            tops.append(to_rows(m_ref[b, part, :]))
            mass = to_rows(acc_ref[b, part, 128:256])
            upper = rounded(mass)
            high.append(upper)
            low.append(mass - upper)
        o_ref[b, 256:264, :] = stacked(tops + high + low, 8).astype(BF16)
        return c

    lax.fori_loop(0, 8, emit, 0)


def combine(msg_ref, a_ref, s_ref):
    copies = s_ref.shape[0]
    n = msg_ref.shape[0]
    stats = [msg_ref[i, 256:264, :].astype(F32) for i in range(n)]
    sums = []
    for h in range(2):
        tops = [s[h : h + 1] for s in stats]
        totals = [s[2 + h : 3 + h] + s[4 + h : 5 + h] for s in stats]
        top = functools.reduce(jnp.maximum, tops)
        weights = [jnp.exp2(t - top) for t in tops]
        total = sum(w * t for w, t in zip(weights, totals))
        shares = jnp.transpose(stacked([w / total for w in weights], 128))
        out = jnp.zeros((128, 128), F32)
        for i in range(n):
            out = out + shares[:, i : i + 1] * msg_ref[i, 128 * h : 128 * h + 128, :].astype(F32)
        out = out.astype(BF16)
        a_ref[128 * h : 128 * h + 128, :] = out
        square = out.astype(F32) * out.astype(F32)
        upper = square.astype(BF16)
        lower = (square - upper.astype(F32)).astype(BF16)
        ones = jnp.ones((8, 128), BF16)
        sums.append((dot(ones, upper, ((1,), (1,))) + dot(ones, lower, ((1,), (1,))))[0:1])
    both = stacked(sums, 8)
    for i in range(copies):
        s_ref[i] = both


def normalize(a_ref, s_ref, g_ref, q_ref, k_ref, c_ref, v_ref, end_ref, begin_ref):
    n = s_ref.shape[0]
    total = functools.reduce(jnp.add, [s_ref[i] for i in range(n)])
    scale = lax.rsqrt(total * (1.0 / (n * 128)) + EPSILON)
    column = jnp.transpose(jnp.concatenate([scale, jnp.zeros((120, 128), F32)], axis=0))
    for h in range(2):
        part = slice(128 * h, 128 * h + 128)
        v_ref[part, :] = (a_ref[part, :].astype(F32) * column[:, h : h + 1] * g_ref[...]).astype(BF16)
    end_ref[0:144, :] = v_ref[112:256, :]
    end_ref[144:160, :] = q_ref[240:256, :]
    end_ref[160:304, :] = k_ref[112:256, :]
    begin_ref[0:16, :] = v_ref[0:16, :]
    begin_ref[16:160, :] = q_ref[0:144, :]
    begin_ref[160:304, :] = c_ref[0:144, :]
    begin_ref[304:320, :] = k_ref[0:16, :]


def picked(stack, rows):
    lane = lax.broadcasted_iota(jnp.int32, (rows, 128), 1) // GROUP_CH
    out = stack[0:rows]
    for g in range(1, 8):
        out = jnp.where(lane == g, stack[g * rows : (g + 1) * rows], out)
    return out


def banded(bands, data_ref):
    out = []
    for b in range(2):
        out.append(picked(dot(bands[...], data_ref[128 * b : 128 * b + 256, :], ((1,), (0,))), 128))
    tail = jnp.concatenate([bands[128 * g : 128 * g + 16, :] for g in range(8)], axis=0)
    out.append(picked(dot(tail, data_ref[256:512, :], ((1,), (0,))), 16)[0:8])
    return out


def build(f_ref, gain_ref, t_ref, bt_ref, g_ref):
    g_ref[...] = gain_ref[...]
    i = lax.broadcasted_iota(jnp.int32, (128, 128), 0)
    j = lax.broadcasted_iota(jnp.int32, (128, 128), 1)
    taps = f_ref[...].astype(BF16)
    front = dot(taps, (i + j == 128).astype(BF16), ((0,), (0,)))
    first = jnp.where(
        lax.broadcasted_iota(jnp.int32, (8, 128), 1) == 0, dot(taps, (i == 0).astype(BF16), ((0,), (0,))), 0.0
    )
    back = dot(taps, (i == j).astype(BF16), ((0,), (0,)))
    front = jnp.concatenate([front, first], axis=1)
    back = jnp.concatenate([back, jnp.zeros((8, 128), F32)], axis=1)
    for g in range(8):
        row = jnp.broadcast_to(front[g : g + 1, :], (128, 256))
        t_ref[128 * g : 128 * g + 128, :] = pltpu.roll(row, 0, 1, stride=1, stride_axis=0).astype(BF16)
        row = jnp.broadcast_to(back[g : g + 1, :], (128, 256))
        bt_ref[128 * g : 128 * g + 128, :] = pltpu.roll(row, 0, 1, stride=1, stride_axis=0).astype(BF16)


def featurized(x_ref, w_ref, index):
    total = jnp.zeros((392, 128), F32)
    for lag in range(FEAT):
        total = total + w_ref[index, lag : lag + 1, :] * x_ref[16 - lag : 408 - lag, :]
    return rounded(total)


def put(z_ref, x):
    z_ref[0:384, :] = x[0:384].astype(BF16)
    z_ref[384:400, :] = jnp.concatenate([x[384:392], jnp.zeros((8, 128), F32)], axis=0).astype(BF16)
    z_ref[400:512, :] = jnp.zeros((112, 128), BF16)


def finish(
    v_ref, q_ref, k_ref, c_ref, before_ref, after_ref, w_ref, t_ref, bt_ref,
    o_ref, gq_ref, gk_ref, gv_ref,
    x_ref, y_ref, s_ref, e_ref, m_ref, n_ref, a_ref, b_ref, d_ref, h_ref,
):
    y_ref[0:16, :] = before_ref[144:160, :].astype(F32)
    y_ref[16:272, :] = q_ref[...].astype(F32)
    y_ref[272:416, :] = after_ref[16:160, :].astype(F32)
    qf = featurized(y_ref, w_ref, 0)
    e_ref[0:256, :] = c_ref[...].astype(F32)
    e_ref[256:400, :] = after_ref[160:304, :].astype(F32)
    put(n_ref, e_ref[0:392, :] * qf)
    x_ref[0:144, :] = before_ref[160:304, :].astype(F32)
    x_ref[144:400, :] = k_ref[...].astype(F32)
    x_ref[400:416, :] = after_ref[304:320, :].astype(F32)
    kf = featurized(x_ref, w_ref, 1)
    s_ref[0:144, :] = before_ref[0:144, :].astype(F32)
    s_ref[144:400, :] = v_ref[...].astype(F32)
    s_ref[400:416, :] = after_ref[0:16, :].astype(F32)
    vf = featurized(s_ref, w_ref, 2)
    put(m_ref, kf * vf)
    for b, back in enumerate(banded(bt_ref, n_ref)):
        d_ref[128 * b : 128 * b + back.shape[0], :] = back
    for b, signal in enumerate(banded(t_ref, m_ref)):
        part = slice(128 * b, 128 * b + signal.shape[0])
        if b < 2:
            o_ref[part, :] = (qf[part] * signal).astype(BF16)
        a_ref[part, :] = rounded(e_ref[part, :] * signal)
    b_ref[...] = rounded(d_ref[...] * vf[128:392])
    h_ref[...] = rounded(d_ref[...] * kf[128:392])
    for i, (src, dst) in enumerate(((a_ref, gq_ref), (b_ref, gk_ref), (h_ref, gv_ref))):
        total = jnp.zeros((256, 128), F32)
        for lag in range(FEAT):
            total = total + w_ref[i, lag : lag + 1, :] * src[lag : lag + 256, :]
        dst[...] = total.astype(BF16)


def shape(dims, dtype=BF16):
    return jax.ShapeDtypeStruct(dims, dtype)


def call(body, outs, args, scratch=(), specs=None, flops=0, size=1 << 20, limit=8):
    single = not isinstance(outs, (list, tuple))
    return pl.pallas_call(
        body,
        out_shape=outs,
        in_specs=specs or [VM] * len(args),
        out_specs=VM if single else [VM] * len(outs),
        scratch_shapes=list(scratch),
        cost_estimate=pl.CostEstimate(flops=flops, bytes_accessed=size, transcendentals=0),
        compiler_params=pltpu.CompilerParams(vmem_limit_bytes=limit << 20),
    )(*args)


CTX = ("y_hi", "x", "core")
HEAD = ("y_lo", "z")


def neighbour(block, distance):
    n = lax.axis_size(CTX)
    return lax.ppermute(block, CTX, [(i, i + distance) for i in range(n) if 0 <= i + distance < n])


def per_device(q_att, k_att, v_att, norm_gain, hy_q, hy_k, feat_w, mr_filt, cotangent):
    info = jnp.stack([lax.axis_index("y_hi"), lax.axis_index("x"), lax.axis_index("core"), 0]).astype(jnp.int32)
    both = jnp.concatenate([k_att, v_att], axis=0)
    came = []
    for d in (1, 2, 3):
        came.append(lax.ppermute(both, "y_hi", [(i, i + d) for i in range(4 - d)]))
    rows = lax.all_to_all(jnp.broadcast_to(q_att[None], (8, BLOCK, HD)), "x", 0, 0, tiled=True)
    own = jnp.stack([both] + came)
    other = lax.ppermute(own, "core", [(0, 1), (1, 0)])
    bands, back_bands, gain = call(
        build, [shape((1024, 256))] * 2 + [shape((1, 128), F32)], (mr_filt, norm_gain[None]), flops=4 * 10**8
    )
    info, rows, own, other, bands, back_bands, gain = lax.optimization_barrier(
        (info, rows, own, other, bands, back_bands, gain)
    )
    partial = call(
        attend,
        shape((8, 264, 128)),
        (info, rows, own, other),
        [
            pltpu.VMEM((4, 512, 128), BF16),
            pltpu.VMEM((4, 512, 256), BF16),
            pltpu.VMEM((8, 256, 256), F32),
            pltpu.VMEM((8, 256, 128), F32),
            pltpu.VMEM((8, 256, 512), F32),
            pltpu.VMEM((8, 256, 128), F32),
            pltpu.VMEM((256, 256), jnp.int32),
        ],
        specs=[SM, VM, VM, VM],
        flops=4 * 10**9,
        limit=24,
    )
    parts = lax.all_to_all(partial, "x", 0, 0, tiled=True)
    attended, sums = call(combine, [shape((256, 128)), shape((16, 8, 128), F32)], (parts,))
    squares = lax.all_to_all(sums, HEAD, 0, 0, tiled=True)
    value, end, begin = call(
        normalize,
        [shape((256, 128)), shape((304, 128)), shape((320, 128))],
        (attended, squares, gain, hy_q, hy_k, cotangent),
    )
    before = neighbour(end, 1)
    after = neighbour(begin, -1)
    tall = pltpu.VMEM((416, 128), F32)
    return tuple(
        call(
            finish,
            [shape((256, 128))] * 4,
            (value, hy_q, hy_k, cotangent, before, after, feat_w, bands, back_bands),
            [tall] * 4 + [pltpu.VMEM((512, 128), BF16)] * 2 + [pltpu.VMEM((264, 128), F32)] * 4,
        )
    )


def solution(mesh):
    fine = Mesh(mesh.devices.reshape(4, 8, 2, 2, 8), CTX + HEAD)
    tokens = P(CTX, HEAD)
    placed = (tokens, tokens, tokens, P(HEAD), tokens, tokens, P(None, None, HEAD), P(None, HEAD), tokens)
    return jax.shard_map(per_device, mesh=fine, in_specs=placed, out_specs=(tokens,) * 4, check_vma=False)
```
